32 devices in a mesh: row: 8 (over y, x, core), col: 4 (over z).
Axes of the slice: x: 2, y: 2, z: 4, core: 2. Of those that a mesh axis runs over, the one named last changes fastest.
Arguments:
- chol: bfloat16 [3, 6144, 2048], P(None, 'row', 'col'), may hold values from -0.67578125 to 0.67578125
- amps: bfloat16 [9, 2048, 2048], P(None, 'row', 'col'), may hold values from -0.19921875 to 0.19921875
- eps_occ: float32 [3], replicated, may hold values from -2 to -0.5
- eps_vir: float32 [2048], replicated, may hold values from 1 to 8
- pairs: int32 [9, 2], replicated, may hold values from 0 to 2, as said below
Outputs:
- residual: float32 [9, 2048, 2048], P(None, 'row', 'col')
The draws below stay inside these ranges and needn't reach their ends.
Inputs may be any that keep to these rules, and one draw needn't show every extreme that they name: `pairs`: the rows list every ordered pair (i, j) of orbitals 0 to 2 exactly once.
All inputs are finite; a program needn't handle non-finite values.
Results may differ from the reference program's by a relative error of at most 0.0039.
Values may be sent and summed in bfloat16 or wider, within the bound.
A program may use at most 128 MiB of HBM per device.

```python
import jax
import jax.numpy as jnp

NVIR = 2048
NCHOL = 6144
OCC = 3
SLABS = 9


def draw_pairs(key, part):
    order = jax.random.permutation(jax.random.fold_in(key, 17), OCC * OCC).astype(jnp.int32)
    return jnp.stack([order // OCC, order % OCC], axis=1).astype(jnp.int32)


def level_of(rng, extent, shards, least, high):
    factor_of, own = 1.0, jax.random.fold_in(rng, 6)
    for dim, shards_of in shards:
        steps = jnp.exp(jax.random.uniform(jax.random.fold_in(own, dim), (shards_of,), jnp.float32, least / len(shards), high / len(shards)))
        factor_of = factor_of * jnp.repeat(steps, extent[dim] // shards_of).reshape([-1 if axis == dim else 1 for axis in range(len(extent))])
    return factor_of


def noise(key, shape, width, bound, shards=(), kind=jnp.bfloat16):
    gain = level_of(key, shape, shards, -0.22, 0.18) if shards else 1.0
    drawn = jax.random.normal(key, shape, jnp.float32) * width * gain
    return jnp.minimum(jnp.maximum(drawn, -bound), bound).astype(kind)


def setup_inputs(seed: int = 0) -> dict:
    arg_keys = jax.random.split(jax.random.key(seed), 6)
    return {
        "chol": noise(arg_keys[0], (OCC, NCHOL, NVIR), (NCHOL ** -0.25), 0.67578125, ((1, 8), (2, 4))),
        "amps": noise(arg_keys[1], (SLABS, NVIR, NVIR), 0.03, 0.19921875, ((1, 8), (2, 4))),
        "eps_occ": jnp.clip(jax.random.uniform(arg_keys[2], (OCC,), jnp.float32, -2.0, -0.5), -2.0, -0.5),
        "eps_vir": jnp.clip(jax.random.uniform(arg_keys[3], (NVIR,), jnp.float32, 1.0, 8.0), 1.0, 8.0),
        "pairs": draw_pairs(jax.random.fold_in(arg_keys[5], 71), 0),
    }


def tdot(left, right):
    return jnp.dot(left.T, right, preferred_element_type=jnp.float32)


def reference(chol, amps, eps_occ, eps_vir, pairs):
    order = jnp.arange(SLABS, dtype=jnp.int32)
    slot = jnp.zeros((OCC, OCC), jnp.int32).at[pairs[:, 0], pairs[:, 1]].set(order)
    amp = [[amps[slot[k, l]] for l in range(OCC)] for k in range(OCC)]
    coulomb = [[tdot(chol[k], chol[l]) for l in range(OCC)] for k in range(OCC)]
    coulomb_b = [[block.astype(jnp.bfloat16) for block in line] for line in coulomb]
    dressed = []
    for k in range(OCC):
        line = []
        for j in range(OCC):
            total = coulomb[k][j]
            for l in range(OCC):
                total = total + jnp.dot(coulomb_b[k][l], amp[l][j], preferred_element_type=jnp.float32)
            line.append(total)
        dressed.append(line)
    dressed_b = [[block.astype(jnp.bfloat16) for block in line] for line in dressed]
    results = []
    for i in range(OCC):
        for j in range(OCC):
            denom = eps_vir[:, None] + eps_vir[None, :] - eps_occ[i] - eps_occ[j]
            result = denom * amp[i][j].astype(jnp.float32) + dressed[i][j]
            for k in range(OCC):
                result = result + jnp.dot(amp[i][k], dressed_b[k][j], preferred_element_type=jnp.float32)
            results.append(result)
    stacked = jnp.stack(results, axis=0)
    flat_pair = (pairs[:, 0] * OCC + pairs[:, 1]).astype(jnp.int32)
    return jnp.take(stacked, flat_pair, axis=0)
```

```python
import functools

import jax
import jax.numpy as jnp
from jax import lax
from jax.experimental import pallas as pl
from jax.experimental.pallas import tpu as pltpu
from jax.sharding import PartitionSpec as P

F32 = jnp.float32
BF16 = jnp.bfloat16
MESH = pl.DeviceIdType.MESH
SPLIT_ROWS = 8


def remote(src, dst, send, recv, index, row):
    return pltpu.make_async_remote_copy(
        src_ref=src,
        dst_ref=dst,
        send_sem=send.at[index],
        recv_sem=recv.at[index],
        device_id={"row": row},
        device_id_type=MESH,
    )


def gather_kernel(size, x_ref, out_ref, own, local, send, recv):
    me = lax.axis_index("row")
    core = lax.rem(me, 2)
    xbit = lax.rem(me // 2, 2)
    ybit = me // 4
    sib = me + 1 - 2 * core
    xn = me + 2 - 4 * xbit
    yn = me + 4 - 8 * ybit
    far = xn + 4 - 8 * ybit
    half = size // 2

    def part(origin, low, count):
        return out_ref.at[:, pl.ds(pl.multiple_of(origin * size + low, 16), count), :]

    c0 = remote(x_ref, part(me, 0, size), send, recv, 0, xn)
    c1 = remote(x_ref, part(me, 0, size), send, recv, 1, yn)
    c2 = remote(x_ref, part(me, 0, size), send, recv, 2, sib)
    c0.start()
    c1.start()
    c2.start()
    bring = pltpu.make_async_copy(x_ref, own, local.at[0])
    bring.start()
    bring.wait()
    place = pltpu.make_async_copy(own, part(me, 0, size), local.at[1])
    place.start()
    c0.wait_recv()
    c3 = remote(part(xn, 0, half), part(xn, 0, half), send, recv, 3, yn)
    c4 = remote(part(xn, 0, size), part(xn, 0, size), send, recv, 4, sib)
    c3.start()
    c4.start()
    c1.wait_recv()
    c5 = remote(part(yn, half, half), part(yn, half, half), send, recv, 5, xn)
    c6 = remote(part(yn, 0, size), part(yn, 0, size), send, recv, 6, sib)
    c5.start()
    c6.start()
    c3.wait_recv()
    c7 = remote(part(far, 0, half), part(far, 0, half), send, recv, 7, sib)
    c7.start()
    c5.wait_recv()
    c8 = remote(part(far, half, half), part(far, half, half), send, recv, 8, sib)
    c8.start()
    for copy in (c2, c4, c6, c7, c8):
        copy.wait_recv()
    for copy in (c0, c1, c2, c3, c4, c5, c6, c7, c8):
        copy.wait_send()
    place.wait()


def gather_rows(x):
    rows = lax.axis_size("row")
    if rows != SPLIT_ROWS:
        return lax.all_gather(x, "row", axis=1, tiled=True)
    lead, size, width = x.shape
    return pl.pallas_call(
        functools.partial(gather_kernel, size),
        out_shape=jax.ShapeDtypeStruct((lead, rows * size, width), x.dtype),
        in_specs=[pl.BlockSpec(memory_space=pl.ANY)],
        out_specs=pl.BlockSpec(memory_space=pl.ANY),
        scratch_shapes=[
            pltpu.VMEM(x.shape, x.dtype),
            pltpu.SemaphoreType.DMA((2,)),
            pltpu.SemaphoreType.DMA((9,)),
            pltpu.SemaphoreType.DMA((9,)),
        ],
        compiler_params=pltpu.CompilerParams(has_side_effects=True),
        cost_estimate=pl.CostEstimate(flops=0, bytes_accessed=16 * rows * x.size, transcendentals=0),
        name="gather_rows",
    )(x)


def swap_kernel(rows, x_ref, out_ref, own, local, send, recv):
    me = lax.axis_index("row")
    size = x_ref.shape[1]
    width = x_ref.shape[2] // rows

    def piece(dest):
        return x_ref.at[:, :, pl.ds(pl.multiple_of(dest * width, width), width)]

    def place(origin):
        return out_ref.at[:, pl.ds(pl.multiple_of(origin * size, size), size), :]

    copies = []
    for step in range(1, rows):
        dest = lax.rem(me + step, rows)
        copies.append(remote(piece(dest), place(me), send, recv, step, dest))
    for copy in copies:
        copy.start()
    bring = pltpu.make_async_copy(piece(me), own, local.at[0])
    bring.start()
    bring.wait()
    keep = pltpu.make_async_copy(own, place(me), local.at[1])
    keep.start()
    for copy in copies:
        copy.wait_recv()
    for copy in copies:
        copy.wait_send()
    keep.wait()


def swap_rows(x):
    rows = lax.axis_size("row")
    if rows != SPLIT_ROWS:
        return lax.all_to_all(x, "row", split_axis=2, concat_axis=1, tiled=True)
    lead, size, width = x.shape
    return pl.pallas_call(
        functools.partial(swap_kernel, rows),
        out_shape=jax.ShapeDtypeStruct((lead, rows * size, width // rows), x.dtype),
        in_specs=[pl.BlockSpec(memory_space=pl.ANY)],
        out_specs=pl.BlockSpec(memory_space=pl.ANY),
        scratch_shapes=[
            pltpu.VMEM((lead, size, width // rows), x.dtype),
            pltpu.SemaphoreType.DMA((2,)),
            pltpu.SemaphoreType.DMA((rows,)),
            pltpu.SemaphoreType.DMA((rows,)),
        ],
        compiler_params=pltpu.CompilerParams(has_side_effects=True),
        cost_estimate=pl.CostEstimate(flops=0, bytes_accessed=32 * x.size, transcendentals=0),
        name="swap_rows",
    )(x)


def per_device(chol, amps, eps_occ, eps_vir, pairs):
    row_index = lax.axis_index("row")
    col_index = lax.axis_index("col")
    occ, depth, _ = chol.shape
    slabs, tile_rows, tile_cols = amps.shape
    flat_pair = pairs[:, 0] * occ + pairs[:, 1]
    matches = (flat_pair[None, :] == jnp.arange(slabs, dtype=jnp.int32)[:, None]).astype(jnp.int32)
    slot = jnp.sum(matches * jnp.arange(slabs, dtype=jnp.int32)[None, :], axis=1)
    grid = jnp.take(amps, slot, axis=0, mode="clip").reshape(occ, occ, tile_rows, tile_cols)
    wide = jnp.transpose(grid, (0, 2, 1, 3)).reshape(occ, tile_rows, occ * tile_cols)

    half = depth // 2
    first, second = chol[:, :half], chol[:, half:]
    amp_cols = gather_rows(wide)
    rows_of_first = lax.all_gather(first, "col", axis=2, tiled=True)
    later, _ = lax.optimization_barrier((second, amp_cols))
    rows_of_second = lax.all_gather(later, "col", axis=2, tiled=True)

    def dress(part, chol_rows):
        y = lax.dot_general(
            chol_rows, amp_cols, (((0, 2), (0, 1)), ((), ())), preferred_element_type=F32
        )
        own = jnp.transpose(part, (1, 0, 2)).reshape(half, occ * tile_cols)
        y = (y + own.astype(F32)).astype(BF16)
        return swap_rows(chol_rows), gather_rows(y[None])[0]

    def close(chol_cols, y_cols):
        return lax.dot_general(
            chol_cols, y_cols, (((1,), (0,)), ((), ())), preferred_element_type=F32
        )

    cols_of_first, y_first = dress(first, rows_of_first)
    rows_of_second, held, cols_of_first, y_first, second = lax.optimization_barrier(
        (rows_of_second, grid, cols_of_first, y_first, second)
    )
    amp_rows = lax.all_gather(held, "col", axis=3, tiled=True)
    cols_of_second, y_second = dress(second, rows_of_second)
    dressed = close(cols_of_first, y_first) + close(cols_of_second, y_second)
    dressed_cols = gather_rows(dressed.astype(BF16))
    quadratic = lax.dot_general(
        amp_rows,
        dressed_cols.reshape(occ, -1, occ * tile_cols),
        (((1, 3), (0, 1)), ((), ())),
        preferred_element_type=F32,
    )
    eps_rows = lax.dynamic_slice_in_dim(eps_vir, row_index * tile_rows, tile_rows, 0)
    eps_cols = lax.dynamic_slice_in_dim(eps_vir, col_index * tile_cols, tile_cols, 0)
    denom = (
        eps_rows[None, :, None, None]
        + eps_cols[None, None, None, :]
        - eps_occ[:, None, None, None]
        - eps_occ[None, None, :, None]
    )
    amp_float = jnp.transpose(grid, (0, 2, 1, 3)).astype(F32)
    shape = (occ, tile_rows, occ, tile_cols)
    result = denom * amp_float + dressed.reshape(shape) + quadratic.reshape(shape)
    ordered = jnp.transpose(result, (0, 2, 1, 3)).reshape(occ * occ, tile_rows, tile_cols)
    return jnp.take(ordered, flat_pair, axis=0, mode="clip")


def solution(mesh):
    placed = (P(None, "row", "col"), P(None, "row", "col"), P(), P(), P())
    return jax.shard_map(
        per_device, mesh=mesh, in_specs=placed, out_specs=P(None, "row", "col"), check_vma=False
    )
```
